32 devices in a mesh: row: 4 (over y, core), col: 8 (over z, x).
Axes of the slice: x: 2, y: 2, z: 4, core: 2. Of those that a mesh axis runs over, the one named last changes fastest.
Arguments:
- y_blocks: bfloat16 [128, 16, 128, 128], P(('row', 'col')), may hold values from -0.3 to 1.3
- z_blocks: bfloat16 [128, 16, 128, 128], P(('row', 'col')), may hold values from -0.3 to 1.3
- pattern: int32 [128, 16], replicated, may hold values from 0 to 127, as said below
Outputs:
- y_next: bfloat16 [128, 16, 128, 128], P(('row', 'col'))
- z_next: bfloat16 [128, 16, 128, 128], P(('row', 'col'))
The draws below stay inside these ranges and needn't reach their ends.
Inputs may be any that keep to these rules, and one draw needn't show every extreme that they name: `pattern`: block row i = (8 x + y) * 4 + z belongs to the domain (x, y, z) of a periodic grid of 4 x 8 x 4 domains. It lists 16 distinct block columns, among them i itself; every column is the block row of a domain ((x + a) mod 4, (y + b) mod 8, (z + c) mod 4) with (a, b) one of (0, 0), (1, 0), (-1, 0), (0, 1), (0, -1) and -1 <= c <= 2.
All inputs are finite; a program needn't handle non-finite values.
Results may differ from the reference program's by a relative error of at most 0.0052.
Values may be sent and summed in bfloat16 or wider, within the bound.
No kernel may reach another device: no remote copies, remote signals or barrier semaphores. Data moves between devices by JAX's collectives and lax.ppermute only.
A program may use at most 192 MiB of HBM per device.

```python
import jax
import jax.numpy as jnp
import numpy as np
from jax import lax

BS = 128
K = 16
RB = 4
GX = 4
GY = 8
NB = 128


def candidate_table():
    entries = []
    for shift_pair in ((0, 0), (-1, 0), (1, 0), (0, -1), (0, 1)):
        for shift_z in (-1, 0, 1, 2):
            if shift_pair[0] != 0 or shift_pair[1] != 0 or shift_z != 0:
                entries.append([shift_pair[0], shift_pair[1], shift_z])
    return np.array(entries, dtype=np.int32)


def shared_pattern(key):
    base = jax.random.fold_in(key, 7)
    table = candidate_table()
    candidate_count = table.shape[0]
    scores = jax.random.randint(base, (NB, candidate_count), 0, 1 << 20) * candidate_count + jnp.arange(candidate_count, dtype=jnp.int32)[None, :]
    ranking = jnp.argsort(scores, axis=1)[:, :K - 1]
    zero_lane = jnp.zeros((NB, 1), jnp.int32)
    shift_x = jnp.concatenate([zero_lane, jnp.take(jnp.asarray(table[:, 0]), ranking)], axis=1)
    shift_y = jnp.concatenate([zero_lane, jnp.take(jnp.asarray(table[:, 1]), ranking)], axis=1)
    shift_z = jnp.concatenate([zero_lane, jnp.take(jnp.asarray(table[:, 2]), ranking)], axis=1)
    mixing = jax.random.randint(jax.random.fold_in(base, 1), (NB, K), 0, 1 << 20) * K + jnp.arange(K, dtype=jnp.int32)[None, :]
    shuffle = jnp.argsort(mixing, axis=1)
    shift_x = jnp.take_along_axis(shift_x, shuffle, axis=1)
    shift_y = jnp.take_along_axis(shift_y, shuffle, axis=1)
    shift_z = jnp.take_along_axis(shift_z, shuffle, axis=1)
    rows_all = jnp.arange(NB, dtype=jnp.int32)
    row_z = jnp.mod(rows_all, RB)[:, None]
    row_y = jnp.mod(rows_all // RB, GY)[:, None]
    row_x = (rows_all // (RB * GY))[:, None]
    column = (jnp.mod(row_x + shift_x, GX) * GY + jnp.mod(row_y + shift_y, GY)) * RB + jnp.mod(row_z + shift_z, RB)
    return column.astype(jnp.int32)


def noisy_blocks(key, salt):
    noise_key = jax.random.fold_in(key, salt)
    values = 0.05 * jax.random.truncated_normal(noise_key, -5.8, 5.8, (NB, K, BS, BS), jnp.float32)
    pattern = shared_pattern(key)
    diagonal = pattern == jnp.arange(NB, dtype=jnp.int32)[:, None]
    identity = jnp.eye(BS, dtype=jnp.float32)
    values = values + jnp.where(diagonal[:, :, None, None], identity, jnp.float32(0.0))
    return values.astype(jnp.bfloat16)


def draw_y_blocks(key, part):
    return noisy_blocks(key, 11)


def draw_z_blocks(key, part):
    return noisy_blocks(key, 13)


def draw_pattern(key, part):
    return shared_pattern(key)


def setup_inputs(seed: int = 0) -> dict:
    seeds = jax.random.split(jax.random.key(seed), 4)
    return {
        "y_blocks": draw_y_blocks(jax.random.fold_in(seeds[3], 71), 0),
        "z_blocks": draw_z_blocks(jax.random.fold_in(seeds[3], 71), 0),
        "pattern": draw_pattern(jax.random.fold_in(seeds[3], 71), 0),
    }


def sparse_product(factor, other, pattern):
    lane_ids = jnp.arange(pattern.shape[1], dtype=jnp.int32)

    def one_row(inputs):
        factor_row, row_cols = inputs
        partner = jnp.take(other, row_cols, axis=0)
        partner_cols = jnp.take(pattern, row_cols, axis=0)
        matches = partner_cols[:, :, None] == row_cols[None, None, :]
        position = jnp.sum(jnp.where(matches, lane_ids[None, :, None], 0), axis=1).astype(jnp.int32)
        present = jnp.any(matches, axis=1)
        chosen = jnp.take_along_axis(partner, position[:, :, None, None], axis=1)
        chosen = jnp.where(present[:, :, None, None], chosen, jnp.zeros_like(chosen))
        return jnp.einsum("kab,kmbc->mac", factor_row.astype(jnp.float32), chosen.astype(jnp.float32))

    return lax.map(one_row, (factor, pattern), batch_size=16)


def reference(y_blocks, z_blocks, pattern):
    product = sparse_product(z_blocks, y_blocks, pattern)
    diagonal = pattern == jnp.arange(pattern.shape[0], dtype=jnp.int32)[:, None]
    identity = jnp.eye(y_blocks.shape[2], dtype=jnp.float32)
    t_blocks = (1.5 * jnp.where(diagonal[:, :, None, None], identity, jnp.float32(0.0)) - 0.5 * product).astype(jnp.bfloat16)
    y_next = sparse_product(y_blocks, t_blocks, pattern).astype(jnp.bfloat16)
    z_next = sparse_product(t_blocks, z_blocks, pattern).astype(jnp.bfloat16)
    return y_next, z_next
```

```python
import functools

import jax
import jax.numpy as jnp
from jax import lax
from jax.experimental import pallas as pl
from jax.experimental.pallas import tpu as pltpu
from jax.sharding import PartitionSpec as P


HBM = pl.BlockSpec(memory_space=pl.ANY)
SMEM = pl.BlockSpec(memory_space=pltpu.SMEM)
VMEM = pl.BlockSpec(memory_space=pltpu.VMEM)

OWN, PARTNER, BEYOND, UPPER, LOWER = range(5)


def slot_domains(row_count, col_count):
    coord_x = lax.axis_index("row")
    coord_y = lax.axis_index("col")
    step = 1 - 2 * lax.rem(coord_y, 2)
    partner = coord_y + step
    beyond = lax.rem(coord_y - step + col_count, col_count)
    upper = lax.rem(coord_x + 1, row_count)
    lower = lax.rem(coord_x + row_count - 1, row_count)
    return (
        coord_x * col_count + coord_y,
        coord_x * col_count + partner,
        coord_x * col_count + beyond,
        upper * col_count + coord_y,
        lower * col_count + coord_y,
    )


def pack_body(grid, with_tables, pattern, blocks, *refs):
    row_count, col_count = grid
    rows, lanes, size, _ = blocks.shape
    units = refs[:5]
    if with_tables:
        table, near, dense, in_sem, out_sem = refs[5:]
    else:
        dense, in_sem, out_sem = refs[5:]
    domains = slot_domains(row_count, col_count)
    dense[...] = jnp.zeros(dense.shape, dense.dtype)
    if with_tables:
        for i in range(rows * 5 * rows):
            table[i] = -1
    for z in range(rows):
        for k in range(lanes):
            column = pattern[domains[0] * rows + z, k]
            domain = lax.div(column, rows)
            depth = column - domain * rows
            slot = jnp.int32(OWN)
            for other in range(1, 5):
                slot = jnp.where(domain == domains[other], other, slot)
            if with_tables:
                table[(z * 5 + slot) * rows + depth] = k
            pltpu.make_async_copy(
                blocks.at[z, k],
                dense.at[slot, pl.ds(z * size, size), pl.ds(pl.multiple_of(depth * size, size), size)],
                in_sem,
            ).start()
    if with_tables:
        for i in range(5 * rows * rows):
            near[i] = 0

        @pl.loop(0, lanes)
        def _(k):
            for slot in range(1, 5):
                for z in range(rows):
                    column = pattern[domains[slot] * rows + z, k]
                    domain = lax.div(column, rows)
                    place = (slot * rows + z) * rows + column - domain * rows
                    near[place] = jnp.where(domain == domains[0], 1, near[place])

    pltpu.make_async_copy(blocks, blocks, in_sem).wait()
    copies = [
        pltpu.make_async_copy(dense.at[slot], units[slot], out_sem.at[slot]) for slot in range(5)
    ]
    for copy in copies:
        copy.start()
    for copy in copies:
        copy.wait()


def pack(blocks, pattern, grid, with_tables):
    rows, _, size, _ = blocks.shape
    order = rows * size
    shapes = [jax.ShapeDtypeStruct((order, order), blocks.dtype)] * 5
    specs = [HBM] * 5
    if with_tables:
        shapes = shapes + [jax.ShapeDtypeStruct((5 * rows * rows,), jnp.int32)] * 2
        specs = specs + [SMEM] * 2
    return pl.pallas_call(
        functools.partial(pack_body, grid, with_tables),
        out_shape=shapes,
        in_specs=[SMEM, HBM],
        out_specs=specs,
        scratch_shapes=[
            pltpu.VMEM((5, order, order), blocks.dtype),
            pltpu.SemaphoreType.DMA,
            pltpu.SemaphoreType.DMA((5,)),
        ],
    )(pattern, blocks)


class Stage:
    def __init__(self, loads, table, near, sinks, outs, blocks_sem, size):
        self.loads, self.table, self.near = loads, table, near
        self.sinks, self.outs, self.blocks_sem, self.size = sinks, outs, blocks_sem, size
        self.arrived = set()
        self.pending = []

    def load(self, key):
        copy, buffer = self.loads[key]
        if key not in self.arrived:
            copy.wait()
            self.arrived.add(key)
        return buffer[...]

    def dot(self, left, right):
        left = self.load(left) if isinstance(left, str) else left
        right = self.load(right) if isinstance(right, str) else right
        return jnp.dot(left, right, preferred_element_type=jnp.float32)

    def scaled(self, value, present, diagonal=False):
        size = self.size
        rows = value.shape[0] // size
        bands = []
        for z in range(rows):
            band = []
            for depth in range(rows):
                block = value[z * size : (z + 1) * size, depth * size : (depth + 1) * size]
                block = block * jnp.where(present(z, depth), jnp.float32(-0.5), jnp.float32(0.0))
                if diagonal and z == depth:
                    r = lax.broadcasted_iota(jnp.int32, (size, size), 0)
                    c = lax.broadcasted_iota(jnp.int32, (size, size), 1)
                    block = block + jnp.where(r == c, jnp.float32(1.5), jnp.float32(0.0))
                band.append(block)
            bands.append(jnp.concatenate(band, axis=1))
        return jnp.concatenate(bands, axis=0).astype(jnp.bfloat16)

    def own_present(self, slot, rows):
        return lambda z, depth: self.table[(z * 5 + slot) * rows + depth] >= 0

    def near_present(self, slot, rows):
        return lambda z, depth: self.near[(slot * rows + z) * rows + depth] > 0

    def emit(self, sink, slot, staging, value):
        size = self.size
        rows = value.shape[0] // size
        staging[...] = value.astype(staging.dtype)
        target = self.sinks[sink]
        for z in range(rows):
            for depth in range(rows):
                place = self.table[(z * 5 + slot) * rows + depth]
                copy = pltpu.make_async_copy(
                    staging.at[pl.ds(z * size, size), pl.ds(depth * size, size)],
                    target.at[z, jnp.maximum(place, 0)],
                    self.blocks_sem.at[len(self.pending)],
                )

                @pl.when(place >= 0)
                def _(copy=copy):
                    copy.start()

                self.pending.append((place, copy))

    def finish(self):
        for place, copy in self.pending:

            @pl.when(place >= 0)
            def _(copy=copy):
                copy.wait()


def stage_call(body, loads, tables, sinks, outs, sparse_shape, emits, after=()):
    keys, sink_keys, out_keys = list(loads), list(sinks), list(outs)
    known = [key for key in sink_keys if sinks[key] is not None]
    size = sparse_shape.shape[2]
    order = sparse_shape.shape[0] * size
    n_after = len(after)

    def kernel(*refs):
        refs = list(refs)
        take = lambda n: [refs.pop(0) for _ in range(n)]
        sources = take(len(keys))
        table, near = take(2)
        take(len(known))
        take(n_after)
        targets = take(len(sink_keys))
        results = take(len(out_keys))
        buffers = take(len(keys))
        stagings = take(emits)
        in_sem, blocks_sem = take(2)
        pairs = {}
        for i, key in enumerate(keys):
            copy = pltpu.make_async_copy(sources[i], buffers[i], in_sem.at[i])
            copy.start()
            pairs[key] = (copy, buffers[i])
        stage = Stage(
            pairs,
            table,
            near,
            dict(zip(sink_keys, targets)),
            dict(zip(out_keys, results)),
            blocks_sem,
            size,
        )
        body(stage, stagings)
        stage.finish()

    first_sink = len(keys) + 2
    return pl.pallas_call(
        kernel,
        out_shape=[sparse_shape] * len(sink_keys) + [outs[key] for key in out_keys],
        in_specs=[HBM] * len(keys) + [SMEM] * 2 + [HBM] * len(known) + [HBM] * n_after,
        out_specs=[HBM] * len(sink_keys) + [VMEM] * len(out_keys),
        scratch_shapes=[pltpu.VMEM(loads[key].shape, loads[key].dtype) for key in keys]
        + [pltpu.VMEM((order, order), sparse_shape.dtype)] * emits
        + [
            pltpu.SemaphoreType.DMA((len(keys),)),
            pltpu.SemaphoreType.DMA((max(1, emits * sparse_shape.shape[0] ** 2),)),
        ],
        input_output_aliases={
            first_sink + i: sink_keys.index(key) for i, key in enumerate(known)
        },
    )(*[loads[key] for key in keys], *tables, *[sinks[key] for key in known], *after)


def on_device(y_blocks, z_blocks, pattern):
    row_count, col_count = lax.axis_size("row"), lax.axis_size("col")
    rows, _, size, _ = y_blocks.shape
    order = rows * size
    grid = (row_count, col_count)
    swap = [(i, i ^ 1) for i in range(col_count)]
    hop = [(i, (i + 2 - 4 * (i % 2)) % col_count) for i in range(col_count)]
    upward = [(i, (i + 1) % row_count) for i in range(row_count)]
    downward = [(i, (i - 1) % row_count) for i in range(row_count)]

    def move(axis, route, value):
        return lax.ppermute(value, axis, route)

    sparse = jax.ShapeDtypeStruct(y_blocks.shape, y_blocks.dtype)
    unit = jax.ShapeDtypeStruct((order, order), y_blocks.dtype)
    sums = jax.ShapeDtypeStruct((order, order), jnp.float32)

    yo, ya, yb, yp, ym = pack(y_blocks, pattern, grid, False)
    yb_seen = move("col", swap, yb)
    y_po = move("row", downward, ym)
    y_mo = move("row", upward, yp)
    y_ao = move("col", swap, ya)
    (z_in, _) = lax.optimization_barrier((z_blocks, yb))
    zo, za, zb, zp, zm, table, near = pack(z_in, pattern, grid, True)
    tables = (table, near)
    zb_seen = move("col", swap, zb)
    y_aa = move("col", swap, yo)
    z_aa = move("col", swap, zo)
    y_pp, z_pp, z_po = (move("row", downward, yo), move("row", downward, zo), move("row", downward, zm))
    y_mm, z_mm, z_mo = (move("row", upward, yo), move("row", upward, zo), move("row", upward, zp))
    y_bo = move("col", hop, yb_seen)

    def own_body(s, stagings):
        value = s.dot("zo", "yo")
        for left, right in (("zp", "y_po"), ("zm", "y_mo"), ("za", "y_ao"), ("zb", "y_bo")):
            value = value + s.dot(left, right)
        s.outs["t"][...] = s.scaled(value, s.own_present(OWN, rows), True)

    (to,) = stage_call(
        own_body,
        dict(zo=zo, yo=yo, zp=zp, y_po=y_po, zm=zm, y_mo=y_mo, za=za, y_ao=y_ao, zb=zb, y_bo=y_bo),
        tables, {}, dict(t=unit), sparse, 0,
    )
    t_aa = move("col", swap, to)
    z_ao = move("col", swap, lax.optimization_barrier((za, to))[0])
    t_pp = move("row", downward, to)
    t_mm = move("row", upward, to)
    z_bo = move("col", hop, zb_seen)
    y_bb = move("col", hop, y_aa)
    z_bb = move("col", hop, z_aa)
    t_bb = move("col", hop, t_aa)

    def edge_body(slot, first, s, stagings):
        t_od = s.scaled(s.dot("zo", "yd") + s.dot("zd", "y_dd"), s.own_present(slot, rows))
        s.outs["t_od"][...] = t_od
        z_next = s.dot("to", "zd") + s.dot(s.outs["t_od"][...], "z_dd")
        s.emit("z", slot, stagings[0], z_next)
        t_do = s.scaled(s.dot("z_do", "yo") + s.dot("z_dd", "y_do"), s.near_present(slot, rows))
        y_sum = s.dot("yo", "to") if first else s.load("y_sum")
        s.outs["y_sum"][...] = y_sum + s.dot("yd", t_do)
        z_sum = s.dot("to", "zo") if first else s.load("z_sum")
        s.outs["z_sum"][...] = z_sum + s.dot(s.outs["t_od"][...], "z_do")

    def edge(slot, yd, zd, y_dd, y_do, z_dd, z_do, z_sink, so_far):
        loads = dict(zo=zo, yd=yd, zd=zd, y_dd=y_dd, to=to, z_dd=z_dd, z_do=z_do, yo=yo, y_do=y_do)
        if so_far:
            loads.update(y_sum=so_far[0], z_sum=so_far[1])
        return stage_call(
            functools.partial(edge_body, slot, not so_far), loads, tables,
            dict(z=z_sink), dict(t_od=unit, y_sum=sums, z_sum=sums), sparse, 1,
        )

    z_next, t_op, y_sum, z_sum = edge(UPPER, yp, zp, y_pp, y_po, z_pp, z_po, None, ())
    z_next, t_om, y_sum, z_sum = edge(LOWER, ym, zm, y_mm, y_mo, z_mm, z_mo, z_next, (y_sum, z_sum))

    def partner_body(s, stagings):
        t_oa = s.scaled(s.dot("zo", "ya") + s.dot("za", "y_aa"), s.own_present(PARTNER, rows))
        s.outs["t_oa"][...] = t_oa
        s.emit("z", PARTNER, stagings[0], s.dot("to", "za") + s.dot(s.outs["t_oa"][...], "z_aa"))

    z_next, t_oa = stage_call(
        partner_body, dict(zo=zo, ya=ya, za=za, y_aa=y_aa, to=to, z_aa=z_aa),
        tables, dict(z=z_next), dict(t_oa=unit), sparse, 1,
    )

    def outer_body(slots, s, stagings):
        for i, slot in enumerate(slots):
            s.emit("y", slot, stagings[i], s.dot("yo", f"t_o{i}") + s.dot(f"y{i}", f"t{i}"))

    (y_next,) = stage_call(
        functools.partial(outer_body, (UPPER, LOWER)),
        dict(yo=yo, t_o0=t_op, y0=yp, t0=t_pp, t_o1=t_om, y1=ym, t1=t_mm),
        tables, dict(y=None), {}, sparse, 2,
    )
    (y_next,) = stage_call(
        functools.partial(outer_body, (PARTNER,)),
        dict(yo=yo, t_o0=t_oa, y0=ya, t0=t_aa), tables, dict(y=y_next), {}, sparse, 1,
    )
    z_next, t_ob, y_sum, z_sum = edge(BEYOND, yb, zb, y_bb, y_bo, z_bb, z_bo, z_next, (y_sum, z_sum))

    def last_body(s, stagings):
        s.emit("y", BEYOND, stagings[0], s.dot("yo", "t_ob") + s.dot("yb", "t_bb"))
        s.emit("z", OWN, stagings[1], s.load("z_sum") + s.dot("t_oa", "z_ao"))
        t_ao = s.scaled(s.dot("z_ao", "yo") + s.dot("z_aa", "y_ao"), s.near_present(PARTNER, rows))
        s.emit("y", OWN, stagings[2], s.load("y_sum") + s.dot("ya", t_ao))

    y_next, z_next = stage_call(
        last_body,
        dict(yo=yo, t_ob=t_ob, yb=yb, t_bb=t_bb, t_oa=t_oa, z_ao=z_ao, z_sum=z_sum, z_aa=z_aa, y_ao=y_ao, ya=ya, y_sum=y_sum),
        tables, dict(y=y_next, z=z_next), {}, sparse, 3,
    )
    return y_next, z_next


def solution(mesh):
    spec = P(("row", "col"), None, None, None)

    return jax.shard_map(on_device, mesh=mesh, in_specs=(spec, spec, P()), out_specs=(spec, spec), check_vma=False)
```

```python
import functools

import jax
import jax.numpy as jnp
from jax import lax
from jax.experimental import pallas as pl
from jax.experimental.pallas import tpu as pltpu
from jax.sharding import PartitionSpec as P


HBM = pl.BlockSpec(memory_space=pltpu.HBM)
SMEM = pl.BlockSpec(memory_space=pltpu.SMEM)
VMEM = pl.BlockSpec(memory_space=pltpu.VMEM)
GRANT = 24 << 20

OWN, PARTNER, BEYOND, UPPER, LOWER = range(5)


def slot_domains(row_count, col_count):
    coord_x = lax.axis_index("row")
    coord_y = lax.axis_index("col")
    step = 1 - 2 * lax.rem(coord_y, 2)
    partner = coord_y + step
    beyond = lax.rem(coord_y - step + col_count, col_count)
    upper = lax.rem(coord_x + 1, row_count)
    lower = lax.rem(coord_x + row_count - 1, row_count)
    return (
        coord_x * col_count + coord_y,
        coord_x * col_count + partner,
        coord_x * col_count + beyond,
        upper * col_count + coord_y,
        lower * col_count + coord_y,
    )


def split(column, rows):
    if rows & (rows - 1) == 0:
        return lax.shift_right_logical(column, rows.bit_length() - 1), column & (rows - 1)
    domain = lax.div(column, rows)
    return domain, column - domain * rows


def copy_slots(slots, rows, table, blocks, units, in_sem):
    size = blocks.shape[2]
    todo = []
    for i, slot in enumerate(slots):
        for z in range(rows):
            for depth in range(rows):
                place = table[(z * 5 + slot) * rows + depth]
                where = units[i].at[pl.ds(z * size, size), pl.ds(depth * size, size)]
                copy = pltpu.make_async_copy(
                    blocks.at[z, jnp.maximum(place, 0)], where, in_sem
                )

                @pl.when(place >= 0)
                def _(copy=copy):
                    copy.start()

                @pl.when(place < 0)
                def _(where=where):
                    where[...] = jnp.zeros(where.shape, where.dtype)

                todo.append((place, copy))
    return todo


def finish_slots(todo):
    for place, copy in todo:

        @pl.when(place >= 0)
        def _(copy=copy):
            copy.wait()


def first_pack_body(slots, grid, columns, blocks, *refs):
    rows, lanes = blocks.shape[:2]
    units, (table, in_sem) = refs[: len(slots)], refs[len(slots) :]
    domains = slot_domains(*grid)
    for i in range(rows * 5 * rows):
        table[i] = -1
    for z in range(rows):
        for k in range(lanes):
            domain, depth = split(columns[k, domains[0] * rows + z], rows)
            slot = jnp.int32(OWN)
            for other in range(1, 5):
                slot = jnp.where(domain == domains[other], other, slot)
            table[(z * 5 + slot) * rows + depth] = k
    finish_slots(copy_slots(slots, rows, table, blocks, units, in_sem))


def pack_body(slots, table, blocks, *refs):
    units, (in_sem,) = refs[: len(slots)], refs[len(slots) :]
    finish_slots(copy_slots(slots, blocks.shape[0], table, blocks, units, in_sem))


def near_pack_body(slots, grid, columns, table, blocks, *refs):
    rows, lanes = blocks.shape[:2]
    units, (near, top, bottom, in_sem) = refs[: len(slots)], refs[len(slots) :]
    todo = copy_slots(slots, rows, table, blocks, units, in_sem)
    domains = slot_domains(*grid)
    for i in range(5 * rows * rows):
        near[i] = 0

    @pl.loop(0, lanes)
    def _(k):
        for slot in range(1, 5):
            for z in range(rows):
                domain, depth = split(columns[k, domains[slot] * rows + z], rows)
                place = (slot * rows + z) * rows + depth
                near[place] = jnp.where(domain == domains[0], 1, near[place])

    finish_slots(todo)
    own, half = units[slots.index(OWN)], top.shape[0]
    top[...] = own[:half]
    bottom[...] = own[half:]


def half_of(blocks):
    order = blocks.shape[0] * blocks.shape[2]
    return jax.ShapeDtypeStruct((order // 2, order), blocks.dtype)


def pack(slots, blocks, columns=None, table=None, grid=None):
    rows, _, size, _ = blocks.shape
    order = rows * size
    entries = jax.ShapeDtypeStruct((5 * rows * rows,), jnp.int32)
    if table is None:
        body, operands = functools.partial(first_pack_body, slots, grid), (columns, blocks)
    elif columns is None:
        body, operands = functools.partial(pack_body, slots), (table, blocks)
    else:
        body, operands = functools.partial(near_pack_body, slots, grid), (columns, table, blocks)
    extra = [] if columns is None else [entries]
    halves = [] if columns is None or table is None else [half_of(blocks)] * 2
    return pl.pallas_call(
        body,
        out_shape=[jax.ShapeDtypeStruct((order, order), blocks.dtype)] * len(slots) + extra + halves,
        in_specs=[SMEM] * (len(operands) - 1) + [HBM],
        out_specs=[VMEM] * len(slots) + [SMEM] * len(extra) + [VMEM] * len(halves),
        scratch_shapes=[pltpu.SemaphoreType.DMA],
        compiler_params=pltpu.CompilerParams(vmem_limit_bytes=GRANT),
    )(*operands)


class Stage:
    def __init__(self, loads, table, near, sinks, outs, blocks_sem, size):
        self.loads, self.table, self.near = loads, table, near
        self.sinks, self.outs, self.blocks_sem, self.size = sinks, outs, blocks_sem, size
        self.pending = []

    def load(self, key):
        if key in self.loads:
            return self.loads[key][...]
        return jnp.concatenate([self.loads[key + "_top"][...], self.loads[key + "_low"][...]], axis=0)

    def dot(self, *pairs):
        value = lambda x: self.load(x) if isinstance(x, str) else x[...]
        lefts = [value(left) for left, _ in pairs]
        rights = [value(right) for _, right in pairs]
        left = lefts[0] if len(pairs) == 1 else jnp.concatenate(lefts, axis=1)
        right = rights[0] if len(pairs) == 1 else jnp.concatenate(rights, axis=0)
        return jnp.dot(left, right, preferred_element_type=jnp.float32)

    def scaled(self, value, present, diagonal=False):
        size = self.size
        rows = value.shape[0] // size
        bands = []
        for z in range(rows):
            band = []
            for depth in range(rows):
                block = value[z * size : (z + 1) * size, depth * size : (depth + 1) * size]
                block = block * jnp.where(present(z, depth), jnp.float32(-0.5), jnp.float32(0.0))
                if diagonal and z == depth:
                    r = lax.broadcasted_iota(jnp.int32, (size, size), 0)
                    c = lax.broadcasted_iota(jnp.int32, (size, size), 1)
                    block = block + jnp.where(r == c, jnp.float32(1.5), jnp.float32(0.0))
                band.append(block)
            bands.append(jnp.concatenate(band, axis=1))
        return jnp.concatenate(bands, axis=0).astype(jnp.bfloat16)

    def own_present(self, slot, rows):
        return lambda z, depth: self.table[(z * 5 + slot) * rows + depth] >= 0

    def near_present(self, slot, rows):
        return lambda z, depth: self.near[(slot * rows + z) * rows + depth] > 0

    def emit(self, sink, slot, staging, value):
        size = self.size
        rows = value.shape[0] // size
        staging[...] = value.astype(staging.dtype)
        target = self.sinks[sink]
        for z in range(rows):
            for depth in range(rows):
                place = self.table[(z * 5 + slot) * rows + depth]
                copy = pltpu.make_async_copy(
                    staging.at[pl.ds(z * size, size), pl.ds(depth * size, size)],
                    target.at[z, jnp.maximum(place, 0)],
                    self.blocks_sem.at[len(self.pending)],
                )

                @pl.when(place >= 0)
                def _(copy=copy):
                    copy.start()

                self.pending.append((place, copy))

    def finish(self):
        for place, copy in self.pending:

            @pl.when(place >= 0)
            def _(copy=copy):
                copy.wait()


def stage_call(body, loads, tables, sinks, outs, sparse_shape, emits):
    keys, sink_keys, out_keys = list(loads), list(sinks), list(outs)
    known = [key for key in sink_keys if sinks[key] is not None]
    size = sparse_shape.shape[2]
    order = sparse_shape.shape[0] * size

    def kernel(*refs):
        refs = list(refs)
        take = lambda n: [refs.pop(0) for _ in range(n)]
        sources = take(len(keys))
        table, near = take(2)
        take(len(known))
        targets = take(len(sink_keys))
        results = take(len(out_keys))
        stagings = take(emits)
        (blocks_sem,) = take(1)
        stage = Stage(
            dict(zip(keys, sources)),
            table,
            near,
            dict(zip(sink_keys, targets)),
            dict(zip(out_keys, results)),
            blocks_sem,
            size,
        )
        body(stage, stagings)
        stage.finish()

    first_sink = len(keys) + 2
    return pl.pallas_call(
        kernel,
        out_shape=[sparse_shape] * len(sink_keys) + [outs[key] for key in out_keys],
        in_specs=[VMEM] * len(keys) + [SMEM] * 2 + [HBM] * len(known),
        out_specs=[HBM] * len(sink_keys) + [VMEM] * len(out_keys),
        scratch_shapes=[pltpu.VMEM((order, order), sparse_shape.dtype)] * emits
        + [pltpu.SemaphoreType.DMA((max(1, emits * sparse_shape.shape[0] ** 2),))],
        compiler_params=pltpu.CompilerParams(vmem_limit_bytes=GRANT),
        input_output_aliases={
            first_sink + i: sink_keys.index(key) for i, key in enumerate(known)
        },
    )(*[loads[key] for key in keys], *tables, *[sinks[key] for key in known])


def on_device(y_blocks, z_blocks, pattern):
    row_count, col_count = lax.axis_size("row"), lax.axis_size("col")
    rows, _, size, _ = y_blocks.shape
    order = rows * size
    grid = (row_count, col_count)
    swap = [(i, i ^ 1) for i in range(col_count)]
    hop = [(i, (i + 2 - 4 * (i % 2)) % col_count) for i in range(col_count)]
    upward = [(i, (i + 1) % row_count) for i in range(row_count)]
    downward = [(i, (i - 1) % row_count) for i in range(row_count)]

    def move(axis, route, value):
        return lax.ppermute(value, axis, route)

    sparse = jax.ShapeDtypeStruct(y_blocks.shape, y_blocks.dtype)
    unit = jax.ShapeDtypeStruct((order, order), y_blocks.dtype)
    sums = jax.ShapeDtypeStruct((order, order), jnp.float32)

    columns = pattern.T
    y_blocks = pltpu.with_memory_space_constraint(y_blocks, pltpu.HBM)
    z_blocks = pltpu.with_memory_space_constraint(z_blocks, pltpu.HBM)
    columns = pltpu.with_memory_space_constraint(columns, pltpu.HBM)
    yb, table = pack((BEYOND,), y_blocks, columns=columns, grid=grid)
    yo, yp, ym, ya = pack((OWN, UPPER, LOWER, PARTNER), y_blocks, table=table)
    zb, zo, zp, zm, za, near, zo_top, zo_low = pack(
        (BEYOND, OWN, UPPER, LOWER, PARTNER), z_blocks, columns=columns, table=table, grid=grid
    )
    yb_seen = move("col", swap, yb)
    y_aa = move("col", swap, yo)
    zb_seen = move("col", swap, zb)
    y_ao = move("col", swap, ya)
    z_aa = [move("col", swap, zo_top), move("col", swap, zo_low)]
    y_po, y_mo = move("row", downward, ym), move("row", upward, yp)
    y_pp, y_mm = move("row", downward, yo), move("row", upward, yo)
    z_pp, z_mm = move("row", downward, zo), move("row", upward, zo)
    z_po, z_mo = move("row", downward, zm), move("row", upward, zp)
    y_bo = move("col", hop, yb_seen)
    y_bb = move("col", hop, y_aa)
    z_bo = move("col", hop, zb_seen)
    z_bb = [move("col", hop, z_aa[0]), move("col", hop, z_aa[1])]

    def call(body, loads, sinks, outs, emits):
        loads = dict(loads)
        for key in [key for key in loads if isinstance(loads[key], list)]:
            loads[key + "_top"], loads[key + "_low"] = loads.pop(key)
        return stage_call(body, loads, (table, near), sinks, outs, sparse, emits)

    def outer_body(s, stagings):
        for i, slot in (("p", UPPER), ("m", LOWER), ("a", PARTNER), ("b", BEYOND)):
            value = s.dot(("zo", f"y{i}"), (f"z{i}", f"y_{i}{i}"))
            s.outs[f"t_o{i}"][...] = s.scaled(value, s.own_present(slot, rows))

    t_op, t_om, t_oa, t_ob = call(
        outer_body,
        dict(zo=zo, yp=yp, zp=zp, y_pp=y_pp, ym=ym, zm=zm, y_mm=y_mm, ya=ya, za=za, y_aa=y_aa, yb=yb, zb=zb, y_bb=y_bb),
        {}, dict(t_op=unit, t_om=unit, t_oa=unit, t_ob=unit), 0,
    )

    def own_body(s, stagings):
        value = s.dot(("zo", "yo"), ("zp", "y_po"), ("zm", "y_mo"), ("za", "y_ao"), ("zb", "y_bo"))
        value = s.scaled(value, s.own_present(OWN, rows), True)
        s.outs["t"][...] = value
        s.outs["t_top"][...] = value[: order // 2]
        s.outs["t_low"][...] = value[order // 2 :]

    half = half_of(y_blocks)
    to, to_top, to_low = call(
        own_body,
        dict(zo=zo, yo=yo, zp=zp, y_po=y_po, zm=zm, y_mo=y_mo, za=za, y_ao=y_ao, zb=zb, y_bo=y_bo),
        {}, dict(t=unit, t_top=half, t_low=half), 0,
    )
    t_aa = [move("col", swap, to_top), move("col", swap, to_low)]
    z_ao = move("col", swap, za)
    t_pp, t_mm = move("row", downward, to), move("row", upward, to)
    t_bb = [move("col", hop, t_aa[0]), move("col", hop, t_aa[1])]

    def rows_in_body(s, stagings):
        for i, slot, staging in (("p", UPPER, stagings[0]), ("m", LOWER, stagings[1])):
            value = s.dot((f"z_{i}o", "yo"), (f"z_{i}{i}", f"y_{i}o"))
            staging[...] = s.scaled(value, s.near_present(slot, rows))
        s.outs["y_sum"][...] = s.dot(("yo", "to"), ("yp", stagings[0]), ("ym", stagings[1]))
        s.outs["z_sum"][...] = s.dot(("to", "zo"), ("t_op", "z_po"), ("t_om", "z_mo"))

    y_sum, z_sum = call(
        rows_in_body,
        dict(z_po=z_po, yo=yo, z_pp=z_pp, y_po=y_po, z_mo=z_mo, z_mm=z_mm, y_mo=y_mo, to=to,
             yp=yp, ym=ym, zo=zo, t_op=t_op, t_om=t_om),
        {}, dict(y_sum=sums, z_sum=sums), 2,
    )

    def partner_body(s, stagings):
        s.emit("z", PARTNER, stagings[0], s.dot(("to", "za"), ("t_oa", "z_aa")))
        s.outs["a_sum"][...] = s.dot(("z_aa", "y_ao"))
        s.outs["b_sum"][...] = s.dot(("yo", "t_ob"))

    z_next, a_sum, b_sum = call(
        partner_body,
        dict(to=to, za=za, t_oa=t_oa, z_aa=z_aa, y_ao=y_ao, yo=yo, t_ob=t_ob),
        dict(z=None), dict(a_sum=sums, b_sum=sums), 1,
    )

    def rows_y_body(s, stagings):
        s.emit("y", UPPER, stagings[0], s.dot(("yo", "t_op"), ("yp", "t_pp")))
        s.emit("y", LOWER, stagings[1], s.dot(("yo", "t_om"), ("ym", "t_mm")))

    (y_next,) = call(
        rows_y_body,
        dict(yo=yo, t_op=t_op, yp=yp, t_pp=t_pp, t_om=t_om, ym=ym, t_mm=t_mm), dict(y=None), {}, 2,
    )

    def beyond_body(s, stagings):
        s.emit("z", BEYOND, stagings[0], s.dot(("to", "zb"), ("t_ob", "z_bb")))
        value = s.dot(("z_bo", "yo"), ("z_bb", "y_bo"))
        stagings[1][...] = s.scaled(value, s.near_present(BEYOND, rows))
        s.outs["z_new"][...] = s.load("z_sum") + s.dot(("t_ob", "z_bo"))
        s.outs["y_new"][...] = s.load("y_sum") + s.dot(("yb", stagings[1]))

    z_next, y_sum, z_sum = call(
        beyond_body,
        dict(to=to, zb=zb, t_ob=t_ob, z_bb=z_bb, z_bo=z_bo, yo=yo, y_bo=y_bo, yb=yb, y_sum=y_sum, z_sum=z_sum),
        dict(z=z_next), dict(y_new=sums, z_new=sums), 2,
    )

    def rows_z_body(s, stagings):
        s.emit("z", UPPER, stagings[0], s.dot(("to", "zp"), ("t_op", "z_pp")))
        s.emit("z", LOWER, stagings[1], s.dot(("to", "zm"), ("t_om", "z_mm")))
        s.emit("y", PARTNER, stagings[2], s.dot(("yo", "t_oa"), ("ya", "t_aa")))

    y_next, z_next = call(
        rows_z_body,
        dict(to=to, zp=zp, t_op=t_op, z_pp=z_pp, zm=zm, t_om=t_om, z_mm=z_mm, yo=yo, t_oa=t_oa, ya=ya, t_aa=t_aa),
        dict(y=y_next, z=z_next), {}, 3,
    )

    def last_body(s, stagings):
        value = s.load("a_sum") + s.dot(("z_ao", "yo"))
        stagings[3][...] = s.scaled(value, s.near_present(PARTNER, rows))
        s.emit("z", OWN, stagings[1], s.load("z_sum") + s.dot(("t_oa", "z_ao")))
        s.emit("y", OWN, stagings[2], s.load("y_sum") + s.dot(("ya", stagings[3])))
        s.emit("y", BEYOND, stagings[0], s.load("b_sum") + s.dot(("yb", "t_bb")))

    return call(
        last_body,
        dict(yo=yo, yb=yb, t_bb=t_bb, z_ao=z_ao, a_sum=a_sum, b_sum=b_sum, t_oa=t_oa, z_sum=z_sum, ya=ya, y_sum=y_sum),
        dict(y=y_next, z=z_next), {}, 4,
    )


def solution(mesh):
    spec = P(("row", "col"), None, None, None)

    return jax.shard_map(on_device, mesh=mesh, in_specs=(spec, spec, P()), out_specs=(spec, spec), check_vma=False)
```
